32 devices in a mesh: grp: 4 (over y, core), dev: 8 (over z, x).
Axes of the slice: x: 2, y: 2, z: 4, core: 2. Of those that a mesh axis runs over, the one named last changes fastest.
Arguments:
- densities: bfloat16 [32, 200, 200], P(('grp', 'dev')), may hold values from -0.4375 to 0.4375
- core_hamiltonian: bfloat16 [32, 200, 200], P(('grp', 'dev')), may hold values from -0.21875 to 0.21875
- embedding: bfloat16 [32, 200, 200], P(('grp', 'dev')), may hold values from -0.21875 to 0.21875
- fit_factors: bfloat16 [192, 200, 200], P('dev'), may hold values from -0.059814453 to 0.059814453
- orthogonalizers: bfloat16 [32, 200, 200], P(('grp', 'dev'))
- pairs: int32 [384, 2], replicated, may hold values from 0 to 31, as said below
- assignment: int32 [384], replicated, may hold values from 0 to 7, as said below
- owner_map: int32 [32], replicated, may hold values from 0 to 31, as said below
Outputs:
- slot_energies: float32 [768], P(('grp', 'dev'))
- total: float32 [], replicated
The draws below stay inside these ranges and needn't reach their ends.
Inputs may be any that keep to these rules, and one draw needn't show every extreme that they name: `pairs`: dimer k belongs to group g = k // 96; its first fragment lies in block g, the fragments g * 8 to (g + 1) * 8 - 1, and its second fragment, different from the first, lies in block g or block g + 1 (only block g for the last group). `assignment`: no device receives more than 24 dimers of its group, and in every group some device receives exactly 24. `owner_map`: A permutation of the fragments that maps each block of 8 fragments onto the rows of the same block.
All inputs are finite; a program needn't handle non-finite values.
Results may differ from the reference program's by a relative error of at most 0.0003.
Values may be sent and summed in bfloat16 or wider, within the bound.
A program may use at most 128 MiB of HBM per device.

```python
import jax
import jax.numpy as jnp
from jax import lax

NB = 200
SLOTS = 24
BLOCK = 8
FRAGS = 32
NAUX = 192
DIM_GRP = 96
NDIMERS = 384
SLOT_ALL = 768


def draw_pairs(key, part):
    base = jax.random.fold_in(key, 11)
    key_first, key_next, key_same, key_far = jax.random.split(base, 4)
    group_count = FRAGS // BLOCK
    group_ids = jnp.arange(NDIMERS, dtype=jnp.int32) // DIM_GRP
    first_local = jax.random.randint(key_first, (NDIMERS,), 0, BLOCK, dtype=jnp.int32)
    go_next = (jax.random.randint(key_next, (NDIMERS,), 0, 2, dtype=jnp.int32) == 1) & (group_ids < group_count - 1)
    offset = jax.random.randint(key_same, (NDIMERS,), 0, BLOCK - 1, dtype=jnp.int32)
    same_local = (first_local + 1 + offset) % BLOCK
    next_local = jax.random.randint(key_far, (NDIMERS,), 0, BLOCK, dtype=jnp.int32)
    second = jnp.where(go_next, (group_ids + 1) * BLOCK + next_local, group_ids * BLOCK + same_local)
    first = group_ids * BLOCK + first_local
    return jnp.stack([first, second], axis=1).astype(jnp.int32)


def draw_assignment(key, part):
    group_count = FRAGS // BLOCK
    token_count = BLOCK * SLOTS
    tokens = jnp.arange(token_count, dtype=jnp.int32) // SLOTS
    positions = jnp.arange(token_count, dtype=jnp.int32)

    def one_group(group_key):
        key_busy, key_score, key_perm = jax.random.split(group_key, 3)
        busiest = jax.random.randint(key_busy, (), 0, BLOCK, dtype=jnp.int32)
        scores = jax.random.randint(key_score, (token_count,), 0, 2 ** 20, dtype=jnp.int32)
        ranking = jnp.where(tokens == busiest, positions, token_count + scores * token_count + positions)
        order = jnp.argsort(ranking, stable=True)
        chosen = tokens[order[:DIM_GRP]]
        shuffle = jax.random.permutation(key_perm, DIM_GRP)
        return chosen[shuffle]
    group_keys = jax.random.split(jax.random.fold_in(key, 23), group_count)
    return jax.vmap(one_group)(group_keys).reshape(-1).astype(jnp.int32)


def draw_owner_map(key, part):
    group_count = FRAGS // BLOCK
    group_keys = jax.random.split(jax.random.fold_in(key, 37), group_count)
    perms = jax.vmap(lambda group_key: jax.random.permutation(group_key, BLOCK))(group_keys)
    shifted = perms + jnp.arange(group_count, dtype=jnp.int32)[:, None] * BLOCK
    return shifted.reshape(-1).astype(jnp.int32)


def draw_orthogonalizers(key, part):
    noise_key = jax.random.fold_in(key, 41)
    shape = (FRAGS, NB, NB)
    noise = jax.random.truncated_normal(noise_key, -3.0, 3.0, shape, jnp.float32)
    identity = jnp.eye(NB, dtype=jnp.float32)[None, :, :]
    return (identity + 0.4 * noise / jnp.sqrt(jnp.float32(NB))).astype(jnp.bfloat16)


def shard_levels(own_key, dims, cuts, low, largest):
    def one(position, blocks):
        heights = jax.random.uniform(jax.random.fold_in(jax.random.fold_in(own_key, 6), position), (blocks,), jnp.float32, low / len(cuts), largest / len(cuts))
        return jnp.repeat(jnp.exp(heights), dims[position] // blocks).reshape((-1,) + (1,) * (len(dims) - position - 1))

    loudness = one(*cuts[0])
    for cut in cuts[1:]:
        loudness = loudness * one(*cut)
    return loudness


def gaussian(rng, extent, deviation, limit, cuts=(), kind=jnp.bfloat16):
    entries = deviation * jax.random.normal(rng, extent, jnp.float32)
    if cuts:
        entries = entries * shard_levels(rng, extent, cuts, -0.22, 0.18)
    return jnp.clip(entries, -limit, limit).astype(kind)


def setup_inputs(seed: int = 0) -> dict:
    streams_of = jax.random.split(jax.random.key(seed), 9)
    densities = gaussian(streams_of[0], (FRAGS, NB, NB), NB ** -0.5, 0.4375, ((0, 32),))
    core_hamiltonian = gaussian(streams_of[1], (FRAGS, NB, NB), (4 * NB) ** -0.5, 0.21875, ((0, 32),))
    embedding = gaussian(streams_of[2], (FRAGS, NB, NB), (4 * NB) ** -0.5, 0.21875, ((0, 32),))
    fit_factors = gaussian(streams_of[3], (NAUX, NB, NB), 0.01, 0.059814453, ((0, 8),))
    orthogonalizers = draw_orthogonalizers(jax.random.fold_in(streams_of[8], 71), 0)
    pairs = draw_pairs(jax.random.fold_in(streams_of[8], 71), 0)
    assignment = draw_assignment(jax.random.fold_in(streams_of[8], 71), 0)
    owner_map = draw_owner_map(jax.random.fold_in(streams_of[8], 71), 0)
    return dict(densities=densities, core_hamiltonian=core_hamiltonian, embedding=embedding, fit_factors=fit_factors, orthogonalizers=orthogonalizers, pairs=pairs, assignment=assignment, owner_map=owner_map)


HALF_WIDTH = 4.0


def product(left, right):
    return jnp.dot(left, right, preferred_element_type=jnp.float32)


def dimer_energy(fock_i, fock_j, dens_i, dens_j, ortho_i, ortho_j):
    coupling = (0.5 * (product(fock_i, dens_j) + product(dens_i, fock_j))).astype(jnp.bfloat16)
    upper_left = product(fock_i, ortho_i).astype(jnp.bfloat16)
    upper_right = product(coupling, ortho_j).astype(jnp.bfloat16)
    lower_left = product(coupling.T, ortho_i).astype(jnp.bfloat16)
    lower_right = product(fock_j, ortho_j).astype(jnp.bfloat16)
    top_rows = jnp.concatenate([product(ortho_i.T, upper_left), product(ortho_i.T, upper_right)], axis=1)
    bottom_rows = jnp.concatenate([product(ortho_j.T, lower_left), product(ortho_j.T, lower_right)], axis=1)
    ortho_fock = jnp.concatenate([top_rows, bottom_rows], axis=0)
    size_two = ortho_fock.shape[0]
    half_basis = fock_i.shape[0]
    start = (0.5 * jnp.eye(size_two, dtype=jnp.float32) - ortho_fock / (2.0 * HALF_WIDTH)).astype(jnp.bfloat16)
    square = product(start, start).astype(jnp.bfloat16)
    cube = product(square, start)
    purified = (3.0 * square.astype(jnp.float32) - 2.0 * cube).astype(jnp.bfloat16)
    left_part = jnp.concatenate([product(ortho_i, purified[:half_basis]), product(ortho_j, purified[half_basis:])], axis=0).astype(jnp.bfloat16)
    new_density = jnp.concatenate([product(left_part[:, :half_basis], ortho_i.T), product(left_part[:, half_basis:], ortho_j.T)], axis=1)
    fock_top = jnp.concatenate([fock_i, coupling], axis=1)
    fock_bottom = jnp.concatenate([coupling.T, fock_j], axis=1)
    dimer_fock = jnp.concatenate([fock_top, fock_bottom], axis=0).astype(jnp.float32)
    monomer_i = jnp.sum(dens_i.astype(jnp.float32) * fock_i.astype(jnp.float32))
    monomer_j = jnp.sum(dens_j.astype(jnp.float32) * fock_j.astype(jnp.float32))
    return jnp.sum(new_density * dimer_fock) - monomer_i - monomer_j


def reference(densities, core_hamiltonian, embedding, fit_factors, orthogonalizers, pairs, assignment, owner_map):
    flat_dens = densities.reshape(FRAGS, NB * NB)
    flat_fit = fit_factors.reshape(NAUX, NB * NB)
    coeffs = lax.dot_general(flat_dens, flat_fit, (((1,), (1,)), ((), ())), preferred_element_type=jnp.float32).astype(jnp.bfloat16)
    coulomb = jnp.dot(coeffs, flat_fit, preferred_element_type=jnp.float32).reshape(FRAGS, NB, NB)
    fock_rows = (core_hamiltonian.astype(jnp.float32) + embedding.astype(jnp.float32) + coulomb).astype(jnp.bfloat16)
    row_pairs = owner_map[pairs].astype(jnp.int32)

    def one_dimer(row_pair):
        first_row = row_pair[0]
        second_row = row_pair[1]
        return dimer_energy(fock_rows[first_row], fock_rows[second_row], densities[first_row], densities[second_row], orthogonalizers[first_row], orthogonalizers[second_row])

    energies = lax.map(one_dimer, row_pairs)
    groups = NDIMERS // DIM_GRP
    group_assign = assignment.reshape(groups, DIM_GRP)
    onehot = (group_assign[:, :, None] == jnp.arange(BLOCK, dtype=jnp.int32)[None, None, :]).astype(jnp.int32)
    earlier = jnp.cumsum(onehot, axis=1) - onehot
    rank = jnp.sum(earlier * onehot, axis=2).astype(jnp.int32)
    group_ids = (jnp.arange(NDIMERS, dtype=jnp.int32) // DIM_GRP).astype(jnp.int32)
    slot_index = ((group_ids * BLOCK + assignment) * SLOTS + rank.reshape(-1)).astype(jnp.int32)
    slot_energies = jnp.zeros((SLOT_ALL,), jnp.float32).at[slot_index].set(energies)
    total = jnp.sum(energies)
    return (slot_energies, total)
```

```python
import jax
import jax.numpy as jnp
from jax import lax
from jax.sharding import PartitionSpec as P

SLOTS = 24
F32 = jnp.float32
BF = jnp.bfloat16


def dot(left, right, dims=((1,), (0,))):
    return lax.dot_general(left, right, (dims, ((), ())), preferred_element_type=F32)


def lookup(table, mono, pairs, assignment, owner_map, group, member, members, groups):
    count = pairs.shape[0]
    per_group = count // groups
    rows = members * groups
    frag_ids = jnp.arange(rows, dtype=jnp.int32)
    row_of = lambda frag: jnp.sum(
        jnp.where(frag[:, None] == frag_ids[None, :], owner_map[None, :], 0), axis=1
    )
    first, second = row_of(pairs[:, 0]), row_of(pairs[:, 1])
    column = second - (jnp.arange(count, dtype=jnp.int32) // per_group) * members
    table_rows = jnp.sum(
        jnp.where((first[:, None] == frag_ids[None, :])[:, :, None], table[None, :, :], 0.0), axis=1
    )
    columns = jnp.arange(2 * members, dtype=jnp.int32)
    energies = jnp.sum(jnp.where(column[:, None] == columns[None, :], table_rows, 0.0), axis=1)
    energies = energies + jnp.sum(
        jnp.where(second[:, None] == frag_ids[None, :], mono[None, :], 0.0), axis=1
    )
    start = group * per_group
    mine = lax.dynamic_slice_in_dim(assignment, start, per_group, 0) == member
    mine_count = mine.astype(jnp.int32)
    before = jnp.cumsum(mine_count) - mine_count
    select = mine[None, :] & (before[None, :] == jnp.arange(SLOTS, dtype=jnp.int32)[:, None])
    own = lax.dynamic_slice_in_dim(energies, start, per_group, 0)
    return jnp.sum(jnp.where(select, own[None, :], 0.0), axis=1), jnp.sum(energies)


def on_device(dens, core, embed, fit, ortho, pairs, assignment, owner_map):
    members, groups = lax.axis_size("dev"), lax.axis_size("grp")
    group, member = lax.axis_index("grp"), lax.axis_index("dev")
    basis = dens.shape[1]
    aux = fit.shape[0]
    flat_fit = fit.reshape(aux, basis * basis)
    gathered = lax.all_gather(dens, "dev", axis=0, tiled=True)
    coeffs = dot(gathered.reshape(members, basis * basis), flat_fit, ((1,), (1,))).astype(BF)
    coulomb = lax.psum_scatter(
        dot(coeffs, flat_fit).reshape(members, basis, basis).astype(BF),
        "dev",
        scatter_dimension=0,
        tiled=True,
    ).astype(F32)
    fock = (core.astype(F32) + embed.astype(F32) + coulomb).astype(BF)[0]
    d, x = dens[0], ortho[0]
    v = dot(fock, x).astype(BF)
    u = dot(d, x).astype(BF)
    xf = dot(x, fock, ((0,), (0,))).astype(BF)
    xd = dot(x, d, ((0,), (0,))).astype(BF)
    a = dot(x, v, ((0,), (0,)))
    a_sym = (0.5 * (a + a.T)).astype(BF)
    ab = a.astype(BF)
    mono = (
        0.5 * jnp.trace(a)
        - 0.1875 * jnp.sum(a * a)
        + jnp.sum(dot(ab, ab) * dot(ab, ab, ((1,), (1,)))) / 256.0
        - jnp.sum(d.astype(F32) * fock.astype(F32))
    )
    block = jnp.stack([u, v, a_sym])[None]
    own_pool = lax.all_gather(block, "dev", axis=0, tiled=True)
    route = [(g, (g - 1) % groups) for g in range(groups)]
    next_pool = lax.ppermute(own_pool, "grp", route)
    pool = jnp.concatenate([own_pool, next_pool], axis=0)

    def pair_term(entry):
        u_j, v_j, c_sym = entry[0], entry[1], entry[2]
        b = 0.5 * (dot(xf, u_j) + dot(xd, v_j))
        bb = b.astype(BF)
        left, right, gram = dot(a_sym, bb), dot(bb, c_sym), dot(bb, bb, ((1,), (1,)))
        both = left + right
        quartic = left * left + right * right + both * both + gram * gram
        return jnp.sum(quartic / 128.0 - 0.375 * (b * b))

    terms = lax.map(pair_term, pool)
    line = jnp.concatenate([terms + mono, mono[None]])
    table = lax.all_gather(line[None], ("grp", "dev"), axis=0, tiled=True)
    return lookup(
        table[:, :-1], table[:, -1], pairs, assignment, owner_map, group, member, members, groups
    )


def solution(mesh):
    rows = P(("grp", "dev"), None, None)
    placed = (rows, rows, rows, P("dev", None, None), rows, P(), P(), P())
    return jax.shard_map(
        on_device, mesh=mesh, in_specs=placed, out_specs=(P(("grp", "dev")), P()), check_vma=False
    )
```

```python
import functools

import jax
import jax.numpy as jnp
from jax import lax
from jax.experimental import pallas as pl
from jax.experimental.pallas import tpu as pltpu
from jax.sharding import PartitionSpec as P

SLOTS = 24
F32 = jnp.float32
BF = jnp.bfloat16
MESH = pl.DeviceIdType.MESH
MONO_LANE = 127


def dot(left, right, dims=((1,), (0,))):
    return lax.dot_general(left, right, (dims, ((), ())), preferred_element_type=F32)


def lookup(table, mono, pairs, assignment, owner_map, group, member, members, groups):
    count = pairs.shape[0]
    per_group = count // groups
    rows = members * groups
    frag_ids = jnp.arange(rows, dtype=jnp.int32)
    row_of = lambda frag: jnp.sum(
        jnp.where(frag[:, None] == frag_ids[None, :], owner_map[None, :], 0), axis=1
    )
    first, second = row_of(pairs[:, 0]), row_of(pairs[:, 1])
    column = second - (jnp.arange(count, dtype=jnp.int32) // per_group) * members
    table_rows = jnp.sum(
        jnp.where((first[:, None] == frag_ids[None, :])[:, :, None], table[None, :, :], 0.0), axis=1
    )
    columns = jnp.arange(2 * members, dtype=jnp.int32)
    energies = jnp.sum(jnp.where(column[:, None] == columns[None, :], table_rows, 0.0), axis=1)
    energies = energies + jnp.sum(
        jnp.where(second[:, None] == frag_ids[None, :], mono[None, :], 0.0), axis=1
    )
    start = group * per_group
    mine = lax.dynamic_slice_in_dim(assignment, start, per_group, 0) == member
    mine_count = mine.astype(jnp.int32)
    before = jnp.cumsum(mine_count) - mine_count
    select = mine[None, :] & (before[None, :] == jnp.arange(SLOTS, dtype=jnp.int32)[:, None])
    own = lax.dynamic_slice_in_dim(energies, start, per_group, 0)
    return jnp.sum(jnp.where(select, own[None, :], 0.0), axis=1), jnp.sum(energies)


def row_chunks(rows, size=32):
    return [(at, min(size, rows - at)) for at in range(0, rows, size)]


def kernel(
    members, groups, dens, core, embed, fit, ortho, table_out,
    dens_pool, ortho_pool, fock_pool, coef, part, inbox, own, sums, table,
    send, recv, part_send, part_recv, row_send, row_recv,
):
    n, half = members, members // 2
    total = members * groups
    basis, aux = fit.shape[1], fit.shape[0]
    group, member = lax.axis_index("grp"), lax.axis_index("dev")
    me = group * n + member
    partner = member + 1 - 2 * lax.rem(member, 2)
    before = lax.rem(group + groups - 1, groups)
    pools = (dens_pool, ortho_pool, fock_pool)

    def other(k):
        flat = lax.rem(me + k, total)
        return (lax.div(flat, n), lax.rem(flat, n))

    def loop(low, high, step):
        def run(k, carry):
            step(k)
            return carry

        lax.fori_loop(low, high, run, 0)

    barrier = pltpu.get_barrier_semaphore()
    loop(
        1,
        total,
        lambda k: pl.semaphore_signal(barrier, inc=1, device_id=other(k), device_id_type=MESH),
    )
    pl.semaphore_wait(barrier, total - 1)

    def remote(src, dst, send_sem, recv_sem, device):
        return pltpu.make_async_remote_copy(
            src_ref=src,
            dst_ref=dst,
            send_sem=send_sem,
            recv_sem=recv_sem,
            device_id=device,
            device_id_type=MESH,
        )

    def ship(m, src, slot, send_slot, device):
        remote(src, pools[m].at[slot], send.at[m, send_slot], recv.at[m, slot], device).start()

    def arrived(m, slot):
        pool = pools[m]
        remote(
            pool.at[slot], pool.at[slot], send.at[m, 0], recv.at[m, slot], (group, partner)
        ).wait_recv()

    def start_own(m, src):
        for k in range(1, half):
            ship(m, src, member, k - 1, (group, lax.rem(member + 2 * k, n)))
        ship(m, src, member, half - 1, (group, partner))
        ship(m, src, n + member, n - 1, (before, member))

    def take_line(m, k):
        slot = lax.rem(member + 2 * k, n)
        arrived(m, slot)
        ship(m, pools[m].at[slot], slot, half - 1 + k, (group, partner))
        ship(m, pools[m].at[slot], n + slot, n - 1 + k, (before, member))
        return slot

    def take_partner(m, k):
        slot = lax.rem(partner + 2 * k, n)
        arrived(m, slot)
        ship(m, pools[m].at[slot], n + slot, n - 1 + half + k, (before, member))
        return slot

    dens_pool[member] = dens[0]
    ortho_pool[member] = ortho[0]
    start_own(0, dens.at[0])
    loop(1, half, lambda k: take_line(0, k))
    start_own(1, ortho.at[0])
    loop(0, half, lambda k: take_partner(0, k))

    def coefficients(p):
        totals = [jnp.zeros((8, basis), F32) for _ in range(n)]
        for at, size in row_chunks(basis):
            factor = fit[p, at : at + size, :].astype(F32)
            for f in range(n):
                prod = dens_pool[f, at : at + size, :].astype(F32) * factor
                totals[f] = totals[f] + jnp.sum(prod.reshape(size // 8, 8, basis), axis=0)
        stacked = jnp.concatenate([jnp.sum(t, axis=0, keepdims=True) for t in totals], axis=0)
        value = jnp.sum(stacked, axis=1, keepdims=True).astype(BF).astype(F32)
        coef[p] = jnp.broadcast_to(value, (n, basis))

    loop(0, aux, coefficients)
    loop(1, half, lambda k: take_line(1, k))

    def partial(slot, at, size):
        value = jnp.zeros((size, basis), F32)
        for p in range(aux):
            value = value + coef[p, pl.ds(slot, 1), :] * fit[p, at : at + size, :].astype(F32)
        return value

    def send_part(k):
        slot = lax.rem(member + k, n)
        for at, size in row_chunks(basis):
            part[k, at : at + size, :] = partial(slot, at, size).astype(BF)
        remote(
            part.at[k], inbox.at[k], part_send.at[k], part_recv.at[k], (group, slot)
        ).start()

    loop(1, n, send_part)
    for at, size in row_chunks(basis):
        sums[at : at + size, :] = (
            partial(member, at, size)
            + core[0, at : at + size, :].astype(F32)
            + embed[0, at : at + size, :].astype(F32)
        )
    loop(0, half, lambda k: take_partner(1, k))

    def add_part(k):
        remote(
            part.at[k], inbox.at[k], part_send.at[k], part_recv.at[k], (group, partner)
        ).wait()
        sums[...] += inbox[k].astype(F32)

    loop(1, n, add_part)
    fock_pool[member] = sums[...].astype(BF)
    start_own(2, fock_pool.at[member])

    fock, d, x = fock_pool[member], dens[0], ortho[0]
    v = dot(fock, x).astype(BF)
    own[0] = (0.5 * dot(x, fock, ((0,), (0,)))).astype(BF)
    own[1] = (0.5 * dot(x, d, ((0,), (0,)))).astype(BF)
    a = dot(x, v, ((0,), (0,)))
    own[2] = (0.5 * (a + a.T)).astype(BF)
    ab = a.astype(BF)
    on_diagonal = lax.broadcasted_iota(jnp.int32, a.shape, 0) == lax.broadcasted_iota(
        jnp.int32, a.shape, 1
    )
    terms = (
        jnp.where(on_diagonal, 0.5 * a, 0.0)
        - 0.1875 * (a * a)
        + dot(ab, ab) * dot(ab, ab, ((1,), (1,))) * (1.0 / 256.0)
        - d.astype(F32) * fock.astype(F32)
    )
    mono = jnp.sum(jnp.sum(terms, axis=0, keepdims=True), axis=1, keepdims=True)

    lanes = lax.broadcasted_iota(jnp.int32, (1, 128), 1)
    table[me] = jnp.where(lanes == MONO_LANE, mono, 0.0)

    def pair(slot):
        x_j = ortho_pool[slot]
        u_j = dot(dens_pool[slot], x_j).astype(BF)
        v_j = dot(fock_pool[slot], x_j).astype(BF)
        c = dot(x_j, v_j, ((0,), (0,)))
        c_sym = (0.5 * (c + c.T)).astype(BF)
        b = dot(own[0], u_j) + dot(own[1], v_j)
        bb = b.astype(BF)
        left, right, gram = dot(own[2], bb), dot(bb, c_sym), dot(bb, bb, ((1,), (1,)))
        both = left + right
        quartic = left * left + right * right + both * both + gram * gram
        terms = quartic * (1.0 / 128.0) - 0.375 * (b * b)
        value = jnp.sum(jnp.sum(terms, axis=0, keepdims=True), axis=1, keepdims=True)
        table[me] = table[me] + jnp.where(lanes == slot, value + mono, 0.0)

    loop(1, half, lambda k: pair(take_line(2, k)))
    loop(0, half, lambda k: pair(take_partner(2, k)))

    def next_pair(k):
        slot = n + lax.rem(member + k, n)
        for m in range(3):
            arrived(m, slot)
        pair(slot)

    loop(0, n, next_pair)

    def send_row(k):
        remote(table.at[me], table.at[me], row_send.at[k], row_recv.at[k], other(k)).start()

    def take_row(k):
        source = lax.rem(me + total - k, total)
        remote(
            table.at[me], table.at[source], row_send.at[k], row_recv.at[k], other(k)
        ).wait()

    loop(1, total, send_row)
    loop(1, total, take_row)
    table_out[...] = table[...]

    def sent(k):
        for m in range(3):
            pool = pools[m]
            remote(
                pool.at[0], pool.at[0], send.at[m, k], recv.at[m, 0], (group, partner)
            ).wait_send()

    loop(0, 2 * n - 1, sent)


def on_device(dens, core, embed, fit, ortho, pairs, assignment, owner_map):
    members, groups = lax.axis_size("dev"), lax.axis_size("grp")
    group, member = lax.axis_index("grp"), lax.axis_index("dev")
    basis, aux = dens.shape[1], fit.shape[0]
    total = members * groups
    square = (basis, basis)
    dma = pltpu.SemaphoreType.DMA
    vmem = pl.BlockSpec(memory_space=pltpu.VMEM)
    table = pl.pallas_call(
        functools.partial(kernel, members, groups),
        out_shape=jax.ShapeDtypeStruct((total, 1, 128), F32),
        in_specs=[vmem] * 5,
        out_specs=vmem,
        scratch_shapes=[
            pltpu.VMEM((2 * members,) + square, BF),
            pltpu.VMEM((2 * members,) + square, BF),
            pltpu.VMEM((2 * members,) + square, BF),
            pltpu.VMEM((aux, members, basis), F32),
            pltpu.VMEM((members,) + square, BF),
            pltpu.VMEM((members,) + square, BF),
            pltpu.VMEM((3,) + square, BF),
            pltpu.VMEM(square, F32),
            pltpu.VMEM((total, 1, 128), F32),
            dma((3, 2 * members - 1)),
            dma((3, 2 * members)),
            dma((members,)),
            dma((members,)),
            dma((total,)),
            dma((total,)),
        ],
        compiler_params=pltpu.CompilerParams(
            collective_id=0, has_side_effects=True, vmem_limit_bytes=60 * 1024 * 1024
        ),
    )(dens, core, embed, fit, ortho)[:, 0]
    return lookup(
        table[:, : 2 * members],
        table[:, MONO_LANE],
        pairs, assignment, owner_map, group, member, members, groups,
    )


def solution(mesh):
    rows = P(("grp", "dev"), None, None)
    placed = (rows, rows, rows, P("dev", None, None), rows, P(), P(), P())
    return jax.shard_map(
        on_device, mesh=mesh, in_specs=placed, out_specs=(P(("grp", "dev")), P()), check_vma=False
    )
```

```python
import functools

import jax
import jax.numpy as jnp
from jax import lax
from jax.experimental import pallas as pl
from jax.experimental.pallas import tpu as pltpu
from jax.sharding import PartitionSpec as P

SLOTS = 24
F32 = jnp.float32
BF = jnp.bfloat16
MESH = pl.DeviceIdType.MESH
MONO_LANE = 127


def dot(left, right, dims=((1,), (0,))):
    return lax.dot_general(left, right, (dims, ((), ())), preferred_element_type=F32)


def lookup(table, mono, pairs, assignment, owner_map, group, member, members, groups):
    count = pairs.shape[0]
    per_group = count // groups
    rows = members * groups
    frag_ids = jnp.arange(rows, dtype=jnp.int32)
    row_of = lambda frag: jnp.sum(
        jnp.where(frag[:, None] == frag_ids[None, :], owner_map[None, :], 0), axis=1
    )
    first, second = row_of(pairs[:, 0]), row_of(pairs[:, 1])
    column = second - (jnp.arange(count, dtype=jnp.int32) // per_group) * members
    table_rows = jnp.sum(
        jnp.where((first[:, None] == frag_ids[None, :])[:, :, None], table[None, :, :], 0.0), axis=1
    )
    columns = jnp.arange(2 * members, dtype=jnp.int32)
    energies = jnp.sum(jnp.where(column[:, None] == columns[None, :], table_rows, 0.0), axis=1)
    energies = energies + jnp.sum(
        jnp.where(second[:, None] == frag_ids[None, :], mono[None, :], 0.0), axis=1
    )
    start = group * per_group
    mine = lax.dynamic_slice_in_dim(assignment, start, per_group, 0) == member
    mine_count = mine.astype(jnp.int32)
    before = jnp.cumsum(mine_count) - mine_count
    select = mine[None, :] & (before[None, :] == jnp.arange(SLOTS, dtype=jnp.int32)[:, None])
    own = lax.dynamic_slice_in_dim(energies, start, per_group, 0)
    return jnp.sum(jnp.where(select, own[None, :], 0.0), axis=1), jnp.sum(energies)


def row_chunks(rows, size=32):
    return [(at, min(size, rows - at)) for at in range(0, rows, size)]


def kernel(
    members, groups, dens, core, embed, fit, ortho, table_out,
    dens_pool, ortho_pool, fock_pool, coef, part, inbox, own, sums, table,
    send, recv, part_send, part_recv, row_send, row_recv,
):
    n, half = members, members // 2
    total = members * groups
    basis, aux = fit.shape[1], fit.shape[0]
    group, member = lax.axis_index("grp"), lax.axis_index("dev")
    me = group * n + member
    place, parity = lax.div(member, 2), lax.rem(member, 2)
    partner = member + 1 - 2 * parity
    before = lax.rem(group + groups - 1, groups)
    pools = (dens_pool, ortho_pool, fock_pool)

    def other(k):
        flat = lax.rem(me + k, total)
        return (lax.div(flat, n), lax.rem(flat, n))

    def loop(low, high, step):
        def run(k, carry):
            step(k)
            return carry

        lax.fori_loop(low, high, run, 0)

    barrier = pltpu.get_barrier_semaphore()
    loop(
        1,
        total,
        lambda k: pl.semaphore_signal(barrier, inc=1, device_id=other(k), device_id_type=MESH),
    )
    pl.semaphore_wait(barrier, total - 1)

    def remote(src, dst, send_sem, recv_sem, device):
        return pltpu.make_async_remote_copy(
            src_ref=src,
            dst_ref=dst,
            send_sem=send_sem,
            recv_sem=recv_sem,
            device_id=device,
            device_id_type=MESH,
        )

    RIGHT, LEFT, PARTNER, BEFORE = 0, 1, 2, 3

    def link(way):
        return (
            (group, member + 2), (group, member - 2), (group, partner), (before, member)
        )[way]

    def copy(m, way, slot, src=None):
        pool = pools[m]
        target = n + slot if way == BEFORE else slot
        return remote(
            pool.at[slot] if src is None else src,
            pool.at[target],
            send.at[m, way, slot],
            recv.at[m, target],
            link(way),
        )

    def arrived(m, slot):
        pool = pools[m]
        remote(
            pool.at[slot], pool.at[slot], send.at[m, PARTNER, 0], recv.at[m, slot], link(PARTNER)
        ).wait_recv()

    has_right, has_left = place < half - 1, place > 0

    def start_own(m, src):
        pl.when(has_right)(lambda: copy(m, RIGHT, member, src).start())
        pl.when(has_left)(lambda: copy(m, LEFT, member, src).start())
        copy(m, PARTNER, member, src).start()
        copy(m, BEFORE, member, src).start()

    def from_left(k, act):
        pl.when(place >= k)(lambda: act(2 * (place - k)))

    def from_right(k, act):
        pl.when(place + k < half)(lambda: act(2 * (place + k)))

    def both_sides(k, left_act, right_act):
        from_left(k, left_act)
        from_right(k, right_act)

    def take_line(m, k):
        def pass_on(slot):
            copy(m, PARTNER, slot).start()
            copy(m, BEFORE, slot).start()

        def left_act(base):
            slot = base + parity
            arrived(m, slot)
            pl.when(has_right)(lambda: copy(m, RIGHT, slot).start())
            pass_on(slot)

        def right_act(base):
            slot = base + parity
            arrived(m, slot)
            pl.when(has_left)(lambda: copy(m, LEFT, slot).start())
            pass_on(slot)

        both_sides(k, left_act, right_act)

    def take_partner(m, k):
        def act(base):
            slot = base + (1 - parity)
            arrived(m, slot)
            copy(m, BEFORE, slot).start()

        if isinstance(k, int) and k == 0:
            act(2 * place)
        else:
            both_sides(k, act, act)

    def take_partners(m):
        take_partner(m, 0)
        loop(1, half, lambda k: take_partner(m, k))

    dens_pool[member] = dens[0]
    ortho_pool[member] = ortho[0]
    start_own(0, dens.at[0])
    loop(1, half, lambda k: take_line(0, k))
    start_own(1, ortho.at[0])
    take_partners(0)

    def coefficients(p):
        totals = [jnp.zeros((8, basis), F32) for _ in range(n)]
        for at, size in row_chunks(basis):
            factor = fit[p, at : at + size, :].astype(F32)
            for f in range(n):
                prod = dens_pool[f, at : at + size, :].astype(F32) * factor
                totals[f] = totals[f] + jnp.sum(prod.reshape(size // 8, 8, basis), axis=0)
        stacked = jnp.concatenate([jnp.sum(t, axis=0, keepdims=True) for t in totals], axis=0)
        value = jnp.sum(stacked, axis=1, keepdims=True).astype(BF).astype(F32)
        coef[p] = jnp.broadcast_to(value, (n, basis))

    loop(0, aux, coefficients)
    loop(1, half, lambda k: take_line(1, k))

    def partial(slot, at, size):
        value = jnp.zeros((size, basis), F32)
        for p in range(aux):
            value = value + coef[p, pl.ds(slot, 1), :] * fit[p, at : at + size, :].astype(F32)
        return value

    def to_partner(line):
        return remote(
            part.at[line], inbox.at[line], part_send.at[line], part_recv.at[line], (group, partner)
        )

    def along(line, arriving):
        return remote(
            part.at[half + line],
            inbox.at[half + arriving],
            part_send.at[half + line],
            part_recv.at[half + arriving],
            (group, 2 * line + parity),
        )

    def give_partner(k):
        line = lax.rem(place + k, half)
        for at, size in row_chunks(basis):
            part[line, at : at + size, :] = partial(2 * line + 1 - parity, at, size).astype(BF)
        to_partner(line).start()

    def give_line(k):
        line = lax.rem(place + k, half)
        to_partner(line).wait_recv()
        for at, size in row_chunks(basis):
            both = partial(2 * line + parity, at, size) + inbox[line, at : at + size, :].astype(F32)
            part[half + line, at : at + size, :] = both.astype(BF)
        along(line, place).start()

    loop(1, half, give_partner)
    give_partner(0)
    loop(1, half, give_line)
    for at, size in row_chunks(basis):
        sums[at : at + size, :] = (
            partial(member, at, size)
            + core[0, at : at + size, :].astype(F32)
            + embed[0, at : at + size, :].astype(F32)
        )
    take_partners(1)
    to_partner(place).wait_recv()
    sums[...] += inbox[place].astype(F32)

    def add_part(k):
        line = lax.rem(place + k, half)
        along(line, line).wait_recv()
        sums[...] += inbox[half + line].astype(F32)

    loop(1, half, add_part)
    fock_pool[member] = sums[...].astype(BF)
    start_own(2, fock_pool.at[member])

    fock, d, x = fock_pool[member], dens[0], ortho[0]
    v = dot(fock, x).astype(BF)
    own[0] = (0.5 * dot(x, fock, ((0,), (0,)))).astype(BF)
    own[1] = (0.5 * dot(x, d, ((0,), (0,)))).astype(BF)
    a = dot(x, v, ((0,), (0,)))
    own[2] = (0.5 * (a + a.T)).astype(BF)
    ab = a.astype(BF)
    on_diagonal = lax.broadcasted_iota(jnp.int32, a.shape, 0) == lax.broadcasted_iota(
        jnp.int32, a.shape, 1
    )
    terms = (
        jnp.where(on_diagonal, 0.5 * a, 0.0)
        - 0.1875 * (a * a)
        + dot(ab, ab) * dot(ab, ab, ((1,), (1,))) * (1.0 / 256.0)
        - d.astype(F32) * fock.astype(F32)
    )
    mono = jnp.sum(jnp.sum(terms, axis=0, keepdims=True), axis=1, keepdims=True)

    lanes = lax.broadcasted_iota(jnp.int32, (1, 128), 1)
    table[me] = jnp.where(lanes == MONO_LANE, mono, 0.0)

    def pair(slot):
        x_j = ortho_pool[slot]
        u_j = dot(dens_pool[slot], x_j).astype(BF)
        v_j = dot(fock_pool[slot], x_j).astype(BF)
        c = dot(x_j, v_j, ((0,), (0,)))
        c_sym = (0.5 * (c + c.T)).astype(BF)
        b = dot(own[0], u_j) + dot(own[1], v_j)
        bb = b.astype(BF)
        left, right, gram = dot(own[2], bb), dot(bb, c_sym), dot(bb, bb, ((1,), (1,)))
        both = left + right
        quartic = left * left + right * right + both * both + gram * gram
        terms = quartic * (1.0 / 128.0) - 0.375 * (b * b)
        value = jnp.sum(jnp.sum(terms, axis=0, keepdims=True), axis=1, keepdims=True)
        table[me] = table[me] + jnp.where(lanes == slot, value + mono, 0.0)

    def line_pairs(k):
        take_line(2, k)
        both_sides(k, lambda base: pair(base + parity), lambda base: pair(base + parity))

    loop(1, half, line_pairs)
    take_partner(2, 0)
    pair(partner)

    def partner_pairs(k):
        take_partner(2, k)
        both_sides(k, lambda base: pair(base + 1 - parity), lambda base: pair(base + 1 - parity))

    loop(1, half, partner_pairs)

    def next_pair(k):
        slot = n + lax.rem(member + k, n)
        for m in range(3):
            arrived(m, slot)
        pair(slot)

    loop(0, n, next_pair)

    def send_row(k):
        remote(table.at[me], table.at[me], row_send.at[k], row_recv.at[k], other(k)).start()

    def take_row(k):
        source = lax.rem(me + total - k, total)
        remote(
            table.at[me], table.at[source], row_send.at[k], row_recv.at[k], other(k)
        ).wait()

    loop(1, total, send_row)
    loop(1, total, take_row)
    table_out[...] = table[...]

    def sent(line):
        slot = 2 * line + parity
        to_partner(line).wait_send()
        pl.when(line != place)(lambda: along(line, line).wait_send())
        for m in range(3):
            pl.when(has_right & (line <= place))(lambda: copy(m, RIGHT, slot).wait_send())
            pl.when(has_left & (line >= place))(lambda: copy(m, LEFT, slot).wait_send())
            copy(m, PARTNER, slot).wait_send()
            copy(m, BEFORE, slot).wait_send()
            copy(m, BEFORE, 2 * line + 1 - parity).wait_send()

    loop(0, half, sent)


def on_device(dens, core, embed, fit, ortho, pairs, assignment, owner_map):
    members, groups = lax.axis_size("dev"), lax.axis_size("grp")
    group, member = lax.axis_index("grp"), lax.axis_index("dev")
    basis, aux = dens.shape[1], fit.shape[0]
    total = members * groups
    square = (basis, basis)
    dma = pltpu.SemaphoreType.DMA
    vmem = pl.BlockSpec(memory_space=pltpu.VMEM)
    table = pl.pallas_call(
        functools.partial(kernel, members, groups),
        out_shape=jax.ShapeDtypeStruct((total, 1, 128), F32),
        in_specs=[vmem] * 5,
        out_specs=vmem,
        scratch_shapes=[
            pltpu.VMEM((2 * members,) + square, BF),
            pltpu.VMEM((2 * members,) + square, BF),
            pltpu.VMEM((2 * members,) + square, BF),
            pltpu.VMEM((aux, members, basis), F32),
            pltpu.VMEM((members,) + square, BF),
            pltpu.VMEM((members,) + square, BF),
            pltpu.VMEM((3,) + square, BF),
            pltpu.VMEM(square, F32),
            pltpu.VMEM((total, 1, 128), F32),
            dma((3, 4, members)),
            dma((3, 2 * members)),
            dma((members,)),
            dma((members,)),
            dma((total,)),
            dma((total,)),
        ],
        compiler_params=pltpu.CompilerParams(
            collective_id=0, has_side_effects=True, vmem_limit_bytes=60 * 1024 * 1024
        ),
    )(dens, core, embed, fit, ortho)[:, 0]
    return lookup(
        table[:, : 2 * members],
        table[:, MONO_LANE],
        pairs, assignment, owner_map, group, member, members, groups,
    )


def solution(mesh):
    rows = P(("grp", "dev"), None, None)
    placed = (rows, rows, rows, P("dev", None, None), rows, P(), P(), P())
    return jax.shard_map(
        on_device, mesh=mesh, in_specs=placed, out_specs=(P(("grp", "dev")), P()), check_vma=False
    )
```

```python
import functools

import jax
import jax.numpy as jnp
from jax import lax
from jax.experimental import pallas as pl
from jax.experimental.pallas import tpu as pltpu
from jax.sharding import PartitionSpec as P

SLOTS = 24
F32 = jnp.float32
BF = jnp.bfloat16
MESH = pl.DeviceIdType.MESH
MONO_LANE = 127


def dot(left, right, dims=((1,), (0,))):
    return lax.dot_general(left, right, (dims, ((), ())), preferred_element_type=F32)


def lookup(table, mono, pairs, assignment, owner_map, group, member, members, groups):
    count = pairs.shape[0]
    per_group = count // groups
    rows = members * groups
    frag_ids = jnp.arange(rows, dtype=jnp.int32)
    row_of = lambda frag: jnp.sum(
        jnp.where(frag[:, None] == frag_ids[None, :], owner_map[None, :], 0), axis=1
    )
    first, second = row_of(pairs[:, 0]), row_of(pairs[:, 1])
    column = second - (jnp.arange(count, dtype=jnp.int32) // per_group) * members
    table_rows = jnp.sum(
        jnp.where((first[:, None] == frag_ids[None, :])[:, :, None], table[None, :, :], 0.0), axis=1
    )
    columns = jnp.arange(2 * members, dtype=jnp.int32)
    energies = jnp.sum(jnp.where(column[:, None] == columns[None, :], table_rows, 0.0), axis=1)
    energies = energies + jnp.sum(
        jnp.where(second[:, None] == frag_ids[None, :], mono[None, :], 0.0), axis=1
    )
    start = group * per_group
    mine = lax.dynamic_slice_in_dim(assignment, start, per_group, 0) == member
    mine_count = mine.astype(jnp.int32)
    before = jnp.cumsum(mine_count) - mine_count
    select = mine[None, :] & (before[None, :] == jnp.arange(SLOTS, dtype=jnp.int32)[:, None])
    own = lax.dynamic_slice_in_dim(energies, start, per_group, 0)
    return jnp.sum(jnp.where(select, own[None, :], 0.0), axis=1), jnp.sum(energies)


def row_chunks(rows, size=32):
    return [(at, min(size, rows - at)) for at in range(0, rows, size)]


def kernel(
    members, groups, dens, core, embed, fit, ortho, table_out,
    dens_pool, ortho_pool, fock_pool, coef, part, inbox, own, sums, table,
    send, recv, part_send, part_recv, row_send, row_recv,
):
    n, half = members, members // 2
    total = members * groups
    basis, aux = fit.shape[1], fit.shape[0]
    group, member = lax.axis_index("grp"), lax.axis_index("dev")
    me = group * n + member
    place, parity = lax.div(member, 2), lax.rem(member, 2)
    partner = member + 1 - 2 * parity
    before = lax.rem(group + groups - 1, groups)
    pools = (dens_pool, ortho_pool, fock_pool)

    def other(k):
        flat = lax.rem(me + k, total)
        return (lax.div(flat, n), lax.rem(flat, n))

    def loop(low, high, step):
        def run(k, carry):
            step(k)
            return carry

        lax.fori_loop(low, high, run, 0)

    barrier = pltpu.get_barrier_semaphore()
    loop(
        1,
        total,
        lambda k: pl.semaphore_signal(barrier, inc=1, device_id=other(k), device_id_type=MESH),
    )
    pl.semaphore_wait(barrier, total - 1)

    def remote(src, dst, send_sem, recv_sem, device):
        return pltpu.make_async_remote_copy(
            src_ref=src,
            dst_ref=dst,
            send_sem=send_sem,
            recv_sem=recv_sem,
            device_id=device,
            device_id_type=MESH,
        )

    RIGHT, LEFT, PARTNER, BEFORE = 0, 1, 2, 3

    def link(way):
        return (
            (group, member + 2), (group, member - 2), (group, partner), (before, member)
        )[way]

    def copy(m, way, slot, src=None):
        pool = pools[m]
        target = n + slot if way == BEFORE else slot
        return remote(
            pool.at[slot] if src is None else src,
            pool.at[target],
            send.at[m, way, slot],
            recv.at[m, target],
            link(way),
        )

    def arrived(m, slot):
        pool = pools[m]
        remote(
            pool.at[slot], pool.at[slot], send.at[m, PARTNER, 0], recv.at[m, slot], link(PARTNER)
        ).wait_recv()

    has_right, has_left = place < half - 1, place > 0

    def start_own(m, src, ways=(RIGHT, LEFT, PARTNER, BEFORE)):
        if RIGHT in ways:
            pl.when(has_right)(lambda: copy(m, RIGHT, member, src).start())
            pl.when(has_left)(lambda: copy(m, LEFT, member, src).start())
        for way in ways:
            if way >= PARTNER:
                copy(m, way, member, src).start()

    def from_left(k, act):
        pl.when(place >= k)(lambda: act(2 * (place - k)))

    def from_right(k, act):
        pl.when(place + k < half)(lambda: act(2 * (place + k)))

    def both_sides(k, left_act, right_act):
        from_left(k, left_act)
        from_right(k, right_act)

    def take_line(m, k, partner_too=True):
        def pass_on(slot):
            if partner_too:
                copy(m, PARTNER, slot).start()
            copy(m, BEFORE, slot).start()

        def left_act(base):
            slot = base + parity
            arrived(m, slot)
            pl.when(has_right)(lambda: copy(m, RIGHT, slot).start())
            pass_on(slot)

        def right_act(base):
            slot = base + parity
            arrived(m, slot)
            pl.when(has_left)(lambda: copy(m, LEFT, slot).start())
            pass_on(slot)

        both_sides(k, left_act, right_act)

    def take_partner(m, k):
        def act(base):
            slot = base + (1 - parity)
            arrived(m, slot)
            copy(m, BEFORE, slot).start()

        if isinstance(k, int) and k == 0:
            act(2 * place)
        else:
            both_sides(k, act, act)

    def take_partners(m):
        take_partner(m, 0)
        loop(1, half, lambda k: take_partner(m, k))

    dens_pool[member] = dens[0]
    ortho_pool[member] = ortho[0]
    start_own(0, dens.at[0])
    loop(1, half, lambda k: take_line(0, k))
    start_own(1, ortho.at[0], (RIGHT, LEFT, BEFORE))

    def coefficients(side):
        def step(p):
            totals = [jnp.zeros((8, basis), F32) for _ in range(half)]
            for at, size in row_chunks(basis):
                factor = fit[p, at : at + size, :].astype(F32)
                for line in range(half):
                    prod = dens_pool[2 * line + side, at : at + size, :].astype(F32) * factor
                    totals[line] = totals[line] + jnp.sum(
                        prod.reshape(size // 8, 8, basis), axis=0
                    )
            stacked = jnp.concatenate(
                [jnp.sum(t, axis=0, keepdims=True) for t in totals], axis=0
            )
            value = jnp.sum(stacked, axis=1, keepdims=True).astype(BF).astype(F32)
            coef[side, p] = jnp.broadcast_to(value, (half, basis))

        loop(0, aux, step)

    coefficients(parity)
    loop(1, half, lambda k: take_line(1, k, False))
    take_partners(0)
    coefficients(1 - parity)

    def partial(slot, at, size):
        side, line = lax.rem(slot, 2), lax.div(slot, 2)
        value = jnp.zeros((size, basis), F32)
        for p in range(aux):
            value = value + coef[side, p, pl.ds(line, 1), :] * fit[p, at : at + size, :].astype(F32)
        return value

    def to_partner(line):
        return remote(
            part.at[line], inbox.at[line], part_send.at[line], part_recv.at[line], (group, partner)
        )

    def along(line, arriving):
        return remote(
            part.at[half + line],
            inbox.at[half + arriving],
            part_send.at[half + line],
            part_recv.at[half + arriving],
            (group, 2 * line + parity),
        )

    def give_partner(k):
        line = lax.rem(place + k, half)
        for at, size in row_chunks(basis):
            part[line, at : at + size, :] = partial(2 * line + 1 - parity, at, size).astype(BF)
        to_partner(line).start()

    def give_line(k):
        line = lax.rem(place + k, half)
        to_partner(line).wait_recv()
        for at, size in row_chunks(basis):
            both = partial(2 * line + parity, at, size) + inbox[line, at : at + size, :].astype(F32)
            part[half + line, at : at + size, :] = both.astype(BF)
        along(line, place).start()

    loop(1, half, give_partner)
    give_partner(0)
    start_own(1, ortho.at[0], (PARTNER,))

    def ortho_across(k):
        act = lambda base: copy(1, PARTNER, base + parity).start()
        both_sides(k, act, act)

    loop(1, half, ortho_across)
    loop(1, half, give_line)
    for at, size in row_chunks(basis):
        sums[at : at + size, :] = (
            partial(member, at, size)
            + core[0, at : at + size, :].astype(F32)
            + embed[0, at : at + size, :].astype(F32)
        )
    take_partners(1)
    to_partner(place).wait_recv()
    sums[...] += inbox[place].astype(F32)

    def add_part(k):
        line = lax.rem(place + k, half)
        along(line, line).wait_recv()
        sums[...] += inbox[half + line].astype(F32)

    loop(1, half, add_part)
    fock_pool[member] = sums[...].astype(BF)
    start_own(2, fock_pool.at[member])

    fock, d, x = fock_pool[member], dens[0], ortho[0]
    v = dot(fock, x).astype(BF)
    own[0] = (0.5 * dot(x, fock, ((0,), (0,)))).astype(BF)
    own[1] = (0.5 * dot(x, d, ((0,), (0,)))).astype(BF)
    a = dot(x, v, ((0,), (0,)))
    own[2] = (0.5 * (a + a.T)).astype(BF)
    ab = a.astype(BF)
    on_diagonal = lax.broadcasted_iota(jnp.int32, a.shape, 0) == lax.broadcasted_iota(
        jnp.int32, a.shape, 1
    )
    terms = (
        jnp.where(on_diagonal, 0.5 * a, 0.0)
        - 0.1875 * (a * a)
        + dot(ab, ab) * dot(ab, ab, ((1,), (1,))) * (1.0 / 256.0)
        - d.astype(F32) * fock.astype(F32)
    )
    mono = jnp.sum(jnp.sum(terms, axis=0, keepdims=True), axis=1, keepdims=True)

    lanes = lax.broadcasted_iota(jnp.int32, (1, 128), 1)
    table[me] = jnp.where(lanes == MONO_LANE, mono, 0.0)

    def pair(slot):
        x_j = ortho_pool[slot]
        u_j = dot(dens_pool[slot], x_j).astype(BF)
        v_j = dot(fock_pool[slot], x_j).astype(BF)
        c = dot(x_j, v_j, ((0,), (0,)))
        c_sym = (0.5 * (c + c.T)).astype(BF)
        b = dot(own[0], u_j) + dot(own[1], v_j)
        bb = b.astype(BF)
        left, right, gram = dot(own[2], bb), dot(bb, c_sym), dot(bb, bb, ((1,), (1,)))
        both = left + right
        quartic = left * left + right * right + both * both + gram * gram
        terms = quartic * (1.0 / 128.0) - 0.375 * (b * b)
        value = jnp.sum(jnp.sum(terms, axis=0, keepdims=True), axis=1, keepdims=True)
        table[me] = table[me] + jnp.where(lanes == slot, value + mono, 0.0)

    def line_pairs(k):
        take_line(2, k)
        both_sides(k, lambda base: pair(base + parity), lambda base: pair(base + parity))

    loop(1, half, line_pairs)
    take_partner(2, 0)
    pair(partner)

    def partner_pairs(k):
        take_partner(2, k)
        both_sides(k, lambda base: pair(base + 1 - parity), lambda base: pair(base + 1 - parity))

    loop(1, half, partner_pairs)

    def next_pair(k):
        slot = n + lax.rem(member + k, n)
        for m in range(3):
            arrived(m, slot)
        pair(slot)

    loop(0, n, next_pair)

    def send_row(k):
        remote(table.at[me], table.at[me], row_send.at[k], row_recv.at[k], other(k)).start()

    def take_row(k):
        source = lax.rem(me + total - k, total)
        remote(
            table.at[me], table.at[source], row_send.at[k], row_recv.at[k], other(k)
        ).wait()

    loop(1, total, send_row)
    loop(1, total, take_row)
    table_out[...] = table[...]

    def sent(line):
        slot = 2 * line + parity
        to_partner(line).wait_send()
        pl.when(line != place)(lambda: along(line, line).wait_send())
        for m in range(3):
            pl.when(has_right & (line <= place))(lambda: copy(m, RIGHT, slot).wait_send())
            pl.when(has_left & (line >= place))(lambda: copy(m, LEFT, slot).wait_send())
            copy(m, PARTNER, slot).wait_send()
            copy(m, BEFORE, slot).wait_send()
            copy(m, BEFORE, 2 * line + 1 - parity).wait_send()

    loop(0, half, sent)


def on_device(dens, core, embed, fit, ortho, pairs, assignment, owner_map):
    members, groups = lax.axis_size("dev"), lax.axis_size("grp")
    group, member = lax.axis_index("grp"), lax.axis_index("dev")
    basis, aux = dens.shape[1], fit.shape[0]
    total = members * groups
    square = (basis, basis)
    dma = pltpu.SemaphoreType.DMA
    vmem = pl.BlockSpec(memory_space=pltpu.VMEM)
    table = pl.pallas_call(
        functools.partial(kernel, members, groups),
        out_shape=jax.ShapeDtypeStruct((total, 1, 128), F32),
        in_specs=[vmem] * 5,
        out_specs=vmem,
        scratch_shapes=[
            pltpu.VMEM((2 * members,) + square, BF),
            pltpu.VMEM((2 * members,) + square, BF),
            pltpu.VMEM((2 * members,) + square, BF),
            pltpu.VMEM((2, aux, members // 2, basis), F32),
            pltpu.VMEM((members,) + square, BF),
            pltpu.VMEM((members,) + square, BF),
            pltpu.VMEM((3,) + square, BF),
            pltpu.VMEM(square, F32),
            pltpu.VMEM((total, 1, 128), F32),
            dma((3, 4, members)),
            dma((3, 2 * members)),
            dma((members,)),
            dma((members,)),
            dma((total,)),
            dma((total,)),
        ],
        compiler_params=pltpu.CompilerParams(
            collective_id=0, has_side_effects=True, vmem_limit_bytes=60 * 1024 * 1024
        ),
    )(dens, core, embed, fit, ortho)[:, 0]
    return lookup(
        table[:, : 2 * members],
        table[:, MONO_LANE],
        pairs, assignment, owner_map, group, member, members, groups,
    )


def solution(mesh):
    rows = P(("grp", "dev"), None, None)
    placed = (rows, rows, rows, P("dev", None, None), rows, P(), P(), P())
    return jax.shard_map(
        on_device, mesh=mesh, in_specs=placed, out_specs=(P(("grp", "dev")), P()), check_vma=False
    )
```

```python
import functools

import jax
import jax.numpy as jnp
from jax import lax
from jax.experimental import pallas as pl
from jax.experimental.pallas import tpu as pltpu
from jax.sharding import PartitionSpec as P

SLOTS = 24
F32 = jnp.float32
BF = jnp.bfloat16
MESH = pl.DeviceIdType.MESH
MONO_LANE = 127


def dot(left, right, dims=((1,), (0,))):
    return lax.dot_general(left, right, (dims, ((), ())), preferred_element_type=F32)


def lookup(table, mono, pairs, assignment, owner_map, group, member, members, groups):
    count = pairs.shape[0]
    per_group = count // groups
    rows = members * groups
    frag_ids = jnp.arange(rows, dtype=jnp.int32)
    row_of = lambda frag: jnp.sum(
        jnp.where(frag[:, None] == frag_ids[None, :], owner_map[None, :], 0), axis=1
    )
    first, second = row_of(pairs[:, 0]), row_of(pairs[:, 1])
    column = second - (jnp.arange(count, dtype=jnp.int32) // per_group) * members
    table_rows = jnp.sum(
        jnp.where((first[:, None] == frag_ids[None, :])[:, :, None], table[None, :, :], 0.0), axis=1
    )
    columns = jnp.arange(2 * members, dtype=jnp.int32)
    energies = jnp.sum(jnp.where(column[:, None] == columns[None, :], table_rows, 0.0), axis=1)
    energies = energies + jnp.sum(
        jnp.where(second[:, None] == frag_ids[None, :], mono[None, :], 0.0), axis=1
    )
    start = group * per_group
    mine = lax.dynamic_slice_in_dim(assignment, start, per_group, 0) == member
    mine_count = mine.astype(jnp.int32)
    before = jnp.cumsum(mine_count) - mine_count
    select = mine[None, :] & (before[None, :] == jnp.arange(SLOTS, dtype=jnp.int32)[:, None])
    own = lax.dynamic_slice_in_dim(energies, start, per_group, 0)
    return jnp.sum(jnp.where(select, own[None, :], 0.0), axis=1), jnp.sum(energies)


def row_chunks(rows, size=32):
    return [(at, min(size, rows - at)) for at in range(0, rows, size)]


def kernel(
    members, groups, dens, core, embed, fit, ortho, table_out,
    dens_pool, ortho_pool, fock_pool, coef, part, inbox, own, sums, table,
    send, recv, part_send, part_recv, row_send, row_recv,
):
    n, half = members, members // 2
    total = members * groups
    basis, aux = fit.shape[1], fit.shape[0]
    group, member = lax.axis_index("grp"), lax.axis_index("dev")
    me = group * n + member
    place, parity = lax.div(member, 2), lax.rem(member, 2)
    partner = member + 1 - 2 * parity
    before = lax.rem(group + groups - 1, groups)
    pools = (dens_pool, ortho_pool, fock_pool)

    def other(k):
        flat = lax.rem(me + k, total)
        return (lax.div(flat, n), lax.rem(flat, n))

    def loop(low, high, step):
        def run(k, carry):
            step(k)
            return carry

        lax.fori_loop(low, high, run, 0)

    barrier = pltpu.get_barrier_semaphore()
    loop(
        1,
        total,
        lambda k: pl.semaphore_signal(barrier, inc=1, device_id=other(k), device_id_type=MESH),
    )
    pl.semaphore_wait(barrier, total - 1)

    def remote(src, dst, send_sem, recv_sem, device):
        return pltpu.make_async_remote_copy(
            src_ref=src,
            dst_ref=dst,
            send_sem=send_sem,
            recv_sem=recv_sem,
            device_id=device,
            device_id_type=MESH,
        )

    RIGHT, LEFT, PARTNER, BEFORE = 0, 1, 2, 3

    def link(way):
        return (
            (group, member + 2), (group, member - 2), (group, partner), (before, member)
        )[way]

    def copy(m, way, slot, src=None):
        pool = pools[m]
        target = n + slot if way == BEFORE else slot
        return remote(
            pool.at[slot] if src is None else src,
            pool.at[target],
            send.at[m, way, slot],
            recv.at[m, target],
            link(way),
        )

    def arrived(m, slot):
        pool = pools[m]
        remote(
            pool.at[slot], pool.at[slot], send.at[m, PARTNER, 0], recv.at[m, slot], link(PARTNER)
        ).wait_recv()

    has_right, has_left = place < half - 1, place > 0

    def start_own(m, src, ways=(RIGHT, LEFT, PARTNER, BEFORE)):
        if RIGHT in ways:
            pl.when(has_right)(lambda: copy(m, RIGHT, member, src).start())
            pl.when(has_left)(lambda: copy(m, LEFT, member, src).start())
        for way in ways:
            if way >= PARTNER:
                copy(m, way, member, src).start()

    def from_left(k, act):
        pl.when(place >= k)(lambda: act(2 * (place - k)))

    def from_right(k, act):
        pl.when(place + k < half)(lambda: act(2 * (place + k)))

    def both_sides(k, left_act, right_act):
        from_left(k, left_act)
        from_right(k, right_act)

    def take_line(m, k, partner_too=True):
        def pass_on(slot):
            if partner_too:
                copy(m, PARTNER, slot).start()
            copy(m, BEFORE, slot).start()

        def left_act(base):
            slot = base + parity
            arrived(m, slot)
            pl.when(has_right)(lambda: copy(m, RIGHT, slot).start())
            pass_on(slot)

        def right_act(base):
            slot = base + parity
            arrived(m, slot)
            pl.when(has_left)(lambda: copy(m, LEFT, slot).start())
            pass_on(slot)

        both_sides(k, left_act, right_act)

    def take_partner(m, k):
        def act(base):
            slot = base + (1 - parity)
            arrived(m, slot)
            copy(m, BEFORE, slot).start()

        if isinstance(k, int) and k == 0:
            act(2 * place)
        else:
            both_sides(k, act, act)

    def take_partners(m):
        take_partner(m, 0)
        loop(1, half, lambda k: take_partner(m, k))

    dens_pool[member] = dens[0]
    ortho_pool[member] = ortho[0]
    start_own(0, dens.at[0])
    loop(1, half, lambda k: take_line(0, k))
    start_own(1, ortho.at[0])

    def coefficients(side):
        def step(p):
            totals = [jnp.zeros((8, basis), F32) for _ in range(half)]
            for at, size in row_chunks(basis):
                factor = fit[p, at : at + size, :].astype(F32)
                for line in range(half):
                    prod = dens_pool[2 * line + side, at : at + size, :].astype(F32) * factor
                    totals[line] = totals[line] + jnp.sum(
                        prod.reshape(size // 8, 8, basis), axis=0
                    )
            stacked = jnp.concatenate(
                [jnp.sum(t, axis=0, keepdims=True) for t in totals], axis=0
            )
            value = jnp.sum(stacked, axis=1, keepdims=True).astype(BF).astype(F32)
            coef[side, p] = jnp.broadcast_to(value, (half, basis))

        loop(0, aux, step)

    coefficients(parity)
    loop(1, half, lambda k: take_line(1, k))
    take_partners(0)
    coefficients(1 - parity)

    def partial(slot, at, size):
        side, line = lax.rem(slot, 2), lax.div(slot, 2)
        value = jnp.zeros((size, basis), F32)
        for p in range(aux):
            value = value + coef[side, p, pl.ds(line, 1), :] * fit[p, at : at + size, :].astype(F32)
        return value

    def to_partner(line):
        return remote(
            part.at[line], inbox.at[line], part_send.at[line], part_recv.at[line], (group, partner)
        )

    def along(line, arriving):
        return remote(
            part.at[half + line],
            inbox.at[half + arriving],
            part_send.at[half + line],
            part_recv.at[half + arriving],
            (group, 2 * line + parity),
        )

    def give_partner(k):
        line = lax.rem(place + k, half)
        for at, size in row_chunks(basis):
            part[line, at : at + size, :] = partial(2 * line + 1 - parity, at, size).astype(BF)
        to_partner(line).start()

    def give_line(k):
        line = lax.rem(place + k, half)
        to_partner(line).wait_recv()
        for at, size in row_chunks(basis):
            both = partial(2 * line + parity, at, size) + inbox[line, at : at + size, :].astype(F32)
            part[half + line, at : at + size, :] = both.astype(BF)
        along(line, place).start()

    loop(1, half, give_partner)
    give_partner(0)
    loop(1, half, give_line)
    for at, size in row_chunks(basis):
        sums[at : at + size, :] = (
            partial(member, at, size)
            + core[0, at : at + size, :].astype(F32)
            + embed[0, at : at + size, :].astype(F32)
        )
    to_partner(place).wait_recv()
    sums[...] += inbox[place].astype(F32)

    def add_part(k):
        line = lax.rem(place + k, half)
        along(line, line).wait_recv()
        sums[...] += inbox[half + line].astype(F32)

    loop(1, half, add_part)
    fock_pool[member] = sums[...].astype(BF)
    start_own(2, fock_pool.at[member])
    take_partners(1)

    fock, d, x = fock_pool[member], dens[0], ortho[0]
    v = dot(fock, x).astype(BF)
    own[0] = (0.5 * dot(x, fock, ((0,), (0,)))).astype(BF)
    own[1] = (0.5 * dot(x, d, ((0,), (0,)))).astype(BF)
    a = dot(x, v, ((0,), (0,)))
    own[2] = (0.5 * (a + a.T)).astype(BF)
    ab = a.astype(BF)
    on_diagonal = lax.broadcasted_iota(jnp.int32, a.shape, 0) == lax.broadcasted_iota(
        jnp.int32, a.shape, 1
    )
    terms = (
        jnp.where(on_diagonal, 0.5 * a, 0.0)
        - 0.1875 * (a * a)
        + dot(ab, ab) * dot(ab, ab, ((1,), (1,))) * (1.0 / 256.0)
        - d.astype(F32) * fock.astype(F32)
    )
    mono = jnp.sum(jnp.sum(terms, axis=0, keepdims=True), axis=1, keepdims=True)

    lanes = lax.broadcasted_iota(jnp.int32, (1, 128), 1)
    table[me] = jnp.where(lanes == MONO_LANE, mono, 0.0)

    def pair(slot):
        x_j = ortho_pool[slot]
        u_j = dot(dens_pool[slot], x_j).astype(BF)
        v_j = dot(fock_pool[slot], x_j).astype(BF)
        c = dot(x_j, v_j, ((0,), (0,)))
        c_sym = (0.5 * (c + c.T)).astype(BF)
        b = dot(own[0], u_j) + dot(own[1], v_j)
        bb = b.astype(BF)
        left, right, gram = dot(own[2], bb), dot(bb, c_sym), dot(bb, bb, ((1,), (1,)))
        both = left + right
        quartic = left * left + right * right + both * both + gram * gram
        terms = quartic * (1.0 / 128.0) - 0.375 * (b * b)
        value = jnp.sum(jnp.sum(terms, axis=0, keepdims=True), axis=1, keepdims=True)
        table[me] = table[me] + jnp.where(lanes == slot, value + mono, 0.0)

    def line_pairs(k):
        take_line(2, k)
        both_sides(k, lambda base: pair(base + parity), lambda base: pair(base + parity))

    loop(1, half, line_pairs)
    take_partner(2, 0)
    pair(partner)

    def partner_pairs(k):
        take_partner(2, k)
        both_sides(k, lambda base: pair(base + 1 - parity), lambda base: pair(base + 1 - parity))

    loop(1, half, partner_pairs)

    def next_pair(k):
        slot = n + lax.rem(member + k, n)
        for m in range(3):
            arrived(m, slot)
        pair(slot)

    loop(0, n, next_pair)

    def send_row(k):
        remote(table.at[me], table.at[me], row_send.at[k], row_recv.at[k], other(k)).start()

    def take_row(k):
        source = lax.rem(me + total - k, total)
        remote(
            table.at[me], table.at[source], row_send.at[k], row_recv.at[k], other(k)
        ).wait()

    loop(1, total, send_row)
    loop(1, total, take_row)
    table_out[...] = table[...]

    def sent(line):
        slot = 2 * line + parity
        to_partner(line).wait_send()
        pl.when(line != place)(lambda: along(line, line).wait_send())
        for m in range(3):
            pl.when(has_right & (line <= place))(lambda: copy(m, RIGHT, slot).wait_send())
            pl.when(has_left & (line >= place))(lambda: copy(m, LEFT, slot).wait_send())
            copy(m, PARTNER, slot).wait_send()
            copy(m, BEFORE, slot).wait_send()
            copy(m, BEFORE, 2 * line + 1 - parity).wait_send()

    loop(0, half, sent)


def on_device(dens, core, embed, fit, ortho, pairs, assignment, owner_map):
    members, groups = lax.axis_size("dev"), lax.axis_size("grp")
    group, member = lax.axis_index("grp"), lax.axis_index("dev")
    basis, aux = dens.shape[1], fit.shape[0]
    total = members * groups
    square = (basis, basis)
    dma = pltpu.SemaphoreType.DMA
    vmem = pl.BlockSpec(memory_space=pltpu.VMEM)
    table = pl.pallas_call(
        functools.partial(kernel, members, groups),
        out_shape=jax.ShapeDtypeStruct((total, 1, 128), F32),
        in_specs=[vmem] * 5,
        out_specs=vmem,
        scratch_shapes=[
            pltpu.VMEM((2 * members,) + square, BF),
            pltpu.VMEM((2 * members,) + square, BF),
            pltpu.VMEM((2 * members,) + square, BF),
            pltpu.VMEM((2, aux, members // 2, basis), F32),
            pltpu.VMEM((members,) + square, BF),
            pltpu.VMEM((members,) + square, BF),
            pltpu.VMEM((3,) + square, BF),
            pltpu.VMEM(square, F32),
            pltpu.VMEM((total, 1, 128), F32),
            dma((3, 4, members)),
            dma((3, 2 * members)),
            dma((members,)),
            dma((members,)),
            dma((total,)),
            dma((total,)),
        ],
        compiler_params=pltpu.CompilerParams(
            collective_id=0, has_side_effects=True, vmem_limit_bytes=60 * 1024 * 1024
        ),
    )(dens, core, embed, fit, ortho)[:, 0]
    return lookup(
        table[:, : 2 * members],
        table[:, MONO_LANE],
        pairs, assignment, owner_map, group, member, members, groups,
    )


def solution(mesh):
    rows = P(("grp", "dev"), None, None)
    placed = (rows, rows, rows, P("dev", None, None), rows, P(), P(), P())
    return jax.shard_map(
        on_device, mesh=mesh, in_specs=placed, out_specs=(P(("grp", "dev")), P()), check_vma=False
    )
```
